32 devices in a mesh: dp: 4 (over z), proto: 8 (over y, x, core).
Axes of the slice: x: 2, y: 2, z: 4, core: 2. Of those that a mesh axis runs over, the one named last changes fastest.
Arguments:
- crop_inputs: bfloat16 [4096, 2048], P('dp'), may hold values from -6 to 6
- hidden_weight: bfloat16 [2048, 2048], replicated, may hold values from -0.125 to 0.125
- hidden_bias: float32 [2048], replicated, may hold values from -3 to 3
- out_weight: bfloat16 [2048, 256], replicated, may hold values from -0.125 to 0.125
- out_bias: float32 [256], replicated, may hold values from -3 to 3
- teacher_feat: bfloat16 [4096, 256], P('dp'), may hold values from -12 to 12
- student_protos: bfloat16 [256, 65536], P('dp', 'proto'), may hold values from -0.375 to 0.375
- teacher_protos: bfloat16 [256, 65536], P('dp', 'proto'), may hold values from -12 to 12
Outputs:
- proto_grad: float32 [256, 65536], P('dp', 'proto')
The draws below stay inside these ranges and needn't reach their ends.
All inputs are finite; a program needn't handle non-finite values.
Results may differ from the reference program's by a relative error of at most 0.00048.
Values may be sent and summed in bfloat16 or wider, within the bound.
A program may use at most 192 MiB of HBM per device.

```python
import jax
import jax.numpy as jnp
from jax import lax

HID = 2048
BOT = 256
PROTOS = 65536
ITERS = 3
CROPS = 4096


cluster_count = 16


def cluster_centers(key):
    return jax.random.truncated_normal(jax.random.fold_in(key, 101), -3.0, 3.0, (cluster_count, BOT), jnp.float32)


def draw_teacher_feat(key, part):
    centers = cluster_centers(key)
    member = jax.random.randint(jax.random.fold_in(key, 202), (CROPS,), 0, cluster_count)
    chosen = centers[member]
    jitter = jax.random.truncated_normal(jax.random.fold_in(key, 203), -3.0, 3.0, (CROPS, BOT), jnp.float32)
    strength = jax.random.uniform(jax.random.fold_in(key, 204), (CROPS, 1), jnp.float32, 0.6, 2.1)
    return (strength * chosen + jitter).astype(jnp.bfloat16)


def draw_teacher_protos(key, part):
    centers = cluster_centers(key)
    first = jax.random.randint(jax.random.fold_in(key, 303), (PROTOS,), 0, cluster_count)
    second = jax.random.randint(jax.random.fold_in(key, 304), (PROTOS,), 0, cluster_count)
    member = jnp.minimum(first, second)
    chosen = centers[member]
    jitter = jax.random.truncated_normal(jax.random.fold_in(key, 305), -3.0, 3.0, (PROTOS, BOT), jnp.float32)
    strength = jax.random.uniform(jax.random.fold_in(key, 306), (PROTOS, 1), jnp.float32, 0.6, 2.1)
    return (strength * chosen + jitter).T.astype(jnp.bfloat16)


def block_scale(key, dims, pieces, least, top_value):
    factor_of = 1.0
    for dim, shards_of in pieces:
        heights = jax.random.uniform(jax.random.fold_in(jax.random.fold_in(key, 6), dim), (shards_of,), jnp.float32, least / len(pieces), top_value / len(pieces))
        factor_of = factor_of * jnp.repeat(jnp.exp(heights), dims[dim] // shards_of).reshape((-1,) + (1,) * (len(dims) - 1 - dim))
    return factor_of


def centred(stream_key, shape, spread, bound, pieces=(), dtype=jnp.bfloat16):
    drawn = spread * jax.random.normal(stream_key, shape, jnp.float32)
    if pieces:
        drawn = drawn * block_scale(stream_key, shape, pieces, -0.22, 0.18)
    return jnp.clip(drawn, -bound, bound).astype(dtype)


def setup_inputs(seed: int = 0) -> dict:
    key_list = jax.random.split(jax.random.key(seed), 9)
    crop_inputs = centred(key_list[0], (CROPS, HID), 1.0, 6.0, ((0, 4),))
    hidden_weight = centred(key_list[1], (HID, HID), HID ** -0.5, 0.125)
    hidden_bias = centred(key_list[2], (HID,), 0.5, 3.0, (), jnp.float32)
    out_weight = centred(key_list[3], (HID, BOT), HID ** -0.5, 0.125)
    out_bias = centred(key_list[4], (BOT,), 0.5, 3.0, (), jnp.float32)
    teacher_feat = draw_teacher_feat(jax.random.fold_in(key_list[8], 71), 0)
    student_protos = centred(key_list[6], (BOT, PROTOS), BOT ** -0.5, 0.375, ((0, 4), (1, 8)))
    teacher_protos = draw_teacher_protos(jax.random.fold_in(key_list[8], 71), 0)
    return {"crop_inputs": crop_inputs, "hidden_weight": hidden_weight, "hidden_bias": hidden_bias, "out_weight": out_weight, "out_bias": out_bias, "teacher_feat": teacher_feat, "student_protos": student_protos, "teacher_protos": teacher_protos}


TEACHER_TEMP = 0.07
STUDENT_TEMP = 0.1

def normalize_rows(values):
    return values * lax.rsqrt(lax.optimization_barrier(jnp.sum(values * values, axis=-1, keepdims=True)) + 1e-06)

def column_norm(protos):
    wide = protos.astype(jnp.float32)
    return jnp.sqrt(lax.optimization_barrier(jnp.sum(wide * wide, axis=0)) + 1e-06)

def reference(crop_inputs, hidden_weight, hidden_bias, out_weight, out_bias, teacher_feat, student_protos, teacher_protos):
    hidden = jax.nn.gelu(jnp.dot(crop_inputs, hidden_weight, preferred_element_type=jnp.float32) + hidden_bias, approximate=False).astype(jnp.bfloat16)
    bottle = jnp.dot(hidden, out_weight, preferred_element_type=jnp.float32) + out_bias
    student_z = normalize_rows(bottle).astype(jnp.bfloat16)
    teacher_z = normalize_rows(teacher_feat.astype(jnp.float32)).astype(jnp.bfloat16)
    column_block = min(PROTOS, 4096)
    blocks = PROTOS // column_block
    student_blocks = student_protos.reshape(BOT, blocks, column_block).transpose(1, 0, 2)
    teacher_blocks = teacher_protos.reshape(BOT, blocks, column_block).transpose(1, 0, 2)

    def teacher_block(protos):
        logit = jnp.dot(teacher_z, protos, preferred_element_type=jnp.float32) / column_norm(protos)
        return jnp.exp(logit / TEACHER_TEMP)
    teacher_exp = lax.map(teacher_block, teacher_blocks)
    row_scale = jnp.ones((CROPS,), jnp.float32)
    col_scale = jnp.ones((blocks, column_block), jnp.float32)
    for round_index in range(ITERS):
        col_scale = 1.0 / jnp.einsum('nbk,b->nk', teacher_exp, row_scale, precision=lax.Precision.HIGHEST)
        row_scale = 1.0 / jnp.einsum('nbk,nk->b', teacher_exp, col_scale, precision=lax.Precision.HIGHEST)

    def student_block(protos):
        logit = jnp.dot(student_z, protos, preferred_element_type=jnp.float32) / column_norm(protos)
        return lax.optimization_barrier(jnp.sum(jnp.exp(logit / STUDENT_TEMP), axis=1))
    student_total = lax.optimization_barrier(jnp.sum(lax.map(student_block, student_blocks), axis=0))

    def grad_block(items):
        protos, expo, scale = items
        norm = column_norm(protos)
        logit = jnp.dot(student_z, protos, preferred_element_type=jnp.float32) / norm
        probs = jnp.exp(logit / STUDENT_TEMP) / student_total[:, None]
        targets = expo * row_scale[:, None] * scale[None, :]
        logit_grad = (probs - targets) / STUDENT_TEMP
        low = logit_grad.astype(jnp.bfloat16)
        col_dot = lax.optimization_barrier(jnp.sum(logit_grad * logit, axis=0))
        summed = jnp.dot(student_z.T, low, preferred_element_type=jnp.float32)
        return summed / norm - protos.astype(jnp.float32) * (col_dot / (norm * norm))
    grads = lax.map(grad_block, (student_blocks, teacher_exp, col_scale))
    return grads.transpose(1, 0, 2).reshape(BOT, PROTOS)
```

```python
import functools

import jax
import jax.numpy as jnp
from jax import lax
from jax.experimental import pallas as pl
from jax.experimental.pallas import tpu as pltpu
from jax.sharding import PartitionSpec as P

ITERS = 3
TEACHER_TEMP = 0.07
STUDENT_TEMP = 0.1
LOG2E = 1.4426950408889634
F32 = jnp.float32
BF16 = jnp.bfloat16
MIB = 1024 * 1024


def normalize_rows(values):
    return values * lax.rsqrt(jnp.sum(values * values, axis=-1, keepdims=True) + 1e-06)


def project(inputs, hidden_weight, hidden_bias, out_weight, out_bias):
    hidden = jax.nn.gelu(
        jnp.dot(inputs, hidden_weight, preferred_element_type=F32) + hidden_bias,
        approximate=False,
    ).astype(BF16)
    bottle = jnp.dot(hidden, out_weight, preferred_element_type=F32) + out_bias
    return normalize_rows(bottle).astype(BF16)


def peer(axis, me, step, size):
    return {axis: lax.rem(me + step, size)}


def barrier(groups):
    sem = pltpu.get_barrier_semaphore()
    count = 0
    for axis, me, size in groups:
        for step in range(1, size):
            pl.semaphore_signal(
                sem, inc=1, device_id=peer(axis, me, step, size), device_id_type=pl.DeviceIdType.MESH
            )
            count += 1
    pl.semaphore_wait(sem, count)


def exchange_copies(n, src, dst, send, recv):
    me = lax.axis_index("dp")
    rows, cols = src.shape[0], src.shape[1] // n
    mine = pl.ds(pl.multiple_of(me * rows, rows), rows)
    copies = []
    for step in range(1, n):
        to = lax.rem(me + step, n)
        copies.append(
            pltpu.make_async_remote_copy(
                src_ref=src.at[:, pl.ds(pl.multiple_of(to * cols, cols), cols)],
                dst_ref=dst.at[mine, :],
                send_sem=send.at[step],
                recv_sem=recv.at[step],
                device_id={"dp": to},
                device_id_type=pl.DeviceIdType.MESH,
            )
        )
    own = pltpu.make_async_copy(
        src.at[:, pl.ds(pl.multiple_of(me * cols, cols), cols)], dst.at[mine, :], recv.at[0]
    )
    return copies, own


def exchange_kernel(n, src, dst, send, recv):
    barrier([("dp", lax.axis_index("dp"), n)])
    copies, own = exchange_copies(n, src, dst, send, recv)
    for copy in copies:
        copy.start()
    own.start()
    own.wait()
    for copy in copies:
        copy.wait()


def exchange(n, protos):
    rows, cols = protos.shape
    return pl.pallas_call(
        functools.partial(exchange_kernel, n),
        out_shape=jax.ShapeDtypeStruct((rows * n, cols // n), protos.dtype),
        in_specs=[pl.BlockSpec(memory_space=pl.ANY)],
        out_specs=pl.BlockSpec(memory_space=pl.ANY),
        scratch_shapes=[pltpu.SemaphoreType.DMA((n,)), pltpu.SemaphoreType.DMA((n,))],
        compiler_params=pltpu.CompilerParams(collective_id=0, has_side_effects=True),
        cost_estimate=pl.CostEstimate(flops=0, bytes_accessed=60 * MIB, transcendentals=0),
    )(protos)


def head_kernel(
    n, m, jb, ib,
    z, tp, sp, out,
    exps, tpt, sps, spt, low, stage, acc, tcoef, sinv, colv,
    part, part2, from_proto, from_dp, rows, stot,
    xsend, xrecv, psend, precv, dsend, drecv, osend, orecv,
):
    dp, proto = lax.axis_index("dp"), lax.axis_index("proto")
    bot, cols = tp.shape
    crops = z.shape[0]
    nj, ni = cols // jb, crops // ib
    lanes = 128

    barrier([("dp", dp, n), ("proto", proto, m)])
    copies, own = exchange_copies(n, sp, sps, xsend, xrecv)
    for copy in copies:
        copy.start()
    own.start()

    def jrange(j):
        return pl.ds(pl.multiple_of(j * jb, jb), jb)

    def irange(i):
        return pl.ds(pl.multiple_of(i * ib, ib), ib)

    def prepare(src, dst, coef, factor):
        @pl.loop(0, nj)
        def _(j):
            block = src[:, jrange(j)].T
            dst[jrange(j), :] = block
            wide = block.astype(F32)
            inv = lax.rsqrt(jnp.sum(wide * wide, axis=1, keepdims=True) + 1e-06) * factor
            coef[jrange(j), :] = jnp.broadcast_to(inv, (jb, lanes))

    def dots(protos, i, first):
        return lax.dot_general(
            protos, z[irange(i), first : first + bot], (((1,), (1,)), ((), ())),
            preferred_element_type=F32,
        )

    def fold(values):
        total = values[:, :lanes]
        for k in range(1, ib // lanes):
            total = total + values[:, k * lanes : (k + 1) * lanes]
        return total

    def add_rows(j, slot):
        scale = 1.0 / jnp.sum(acc[...], axis=1, keepdims=True)
        colv[jrange(j), :] = jnp.broadcast_to(scale, (jb, lanes))

        @pl.loop(0, ni)
        def _(i):
            part[slot, pl.ds(i, 1), :] += jnp.sum(
                exps[jrange(j), irange(i)] * scale, axis=0, keepdims=True
            )

    def reduce_copies(axis, me, size, src, dst, send, recv, slot, height):
        return [
            pltpu.make_async_remote_copy(
                src_ref=src.at[slot, pl.ds(0, height), :],
                dst_ref=dst.at[slot, step, pl.ds(0, height), :],
                send_sem=send.at[slot, step],
                recv_sem=recv.at[slot, step],
                device_id=peer(axis, me, step, size),
                device_id_type=pl.DeviceIdType.MESH,
            )
            for step in range(1, size)
        ]

    def reduce_all(slot, height, fillers):
        first = reduce_copies("proto", proto, m, part, from_proto, psend, precv, slot, height)
        for copy in first:
            copy.start()
        fillers[0]()
        for copy in first:
            copy.wait()
        total = part[slot, 0:height, :]
        for step in range(1, m):
            total = total + from_proto[slot, step, 0:height, :]
        part2[slot, 0:height, :] = total
        second = reduce_copies("dp", dp, n, part2, from_dp, dsend, drecv, slot, height)
        for copy in second:
            copy.start()
        fillers[1]()
        for copy in second:
            copy.wait()
        total = part2[slot, 0:height, :]
        for step in range(1, n):
            total = total + from_dp[slot, step, 0:height, :]
        return total

    def nothing():
        pass

    part[...] = jnp.zeros_like(part)
    prepare(tp, tpt, tcoef, LOG2E / TEACHER_TEMP)

    @pl.loop(0, nj)
    def _(j):
        acc[...] = jnp.zeros_like(acc)
        coef = tcoef[jrange(j), 0:1]

        @pl.loop(0, ni)
        def _(i):
            block = jnp.exp2(dots(tpt[jrange(j), :], i, 0) * coef)
            exps[jrange(j), irange(i)] = block
            acc[...] += fold(block)

        add_rows(j, 0)

    def student_totals(first, last):
        @pl.loop(first, last)
        def _(j):
            coef = sinv[jrange(j), 0:1] * (LOG2E / STUDENT_TEMP)

            @pl.loop(0, ni)
            def _(i):
                block = jnp.exp2(dots(spt[jrange(j), :], i, bot) * coef)
                part[2, pl.ds(ni + i, 1), :] += jnp.sum(block, axis=0, keepdims=True)

    def student_first():
        own.wait()
        for copy in copies:
            copy.wait()
        prepare(sps, spt, sinv, 1.0)
        student_totals(0, nj // 2)

    def student_second():
        student_totals(nj // 2, nj)

    for slot in range(ITERS):
        last = slot == ITERS - 1
        fillers = (student_first, student_second) if slot == ITERS - 2 else (nothing, nothing)
        total = reduce_all(slot, 2 * ni if last else ni, fillers)
        rows[...] = 1.0 / total[0:ni, :]
        if last:
            stot[...] = (1.0 / STUDENT_TEMP) / total[ni : 2 * ni, :]
            break

        @pl.loop(0, nj)
        def _(j):
            acc[...] = jnp.zeros_like(acc)

            @pl.loop(0, ni)
            def _(i):
                acc[...] += fold(exps[jrange(j), irange(i)] * rows[pl.ds(i, 1), :])

            add_rows(j, slot + 1)

    height = bot // n
    mine = pl.ds(pl.multiple_of(dp * height, height), height)

    def out_copies(j):
        place = pl.ds(pl.multiple_of(dp * cols + j * jb, jb), jb)
        remote = []
        for step in range(1, n):
            to = lax.rem(dp + step, n)
            remote.append(
                pltpu.make_async_remote_copy(
                    src_ref=stage.at[pl.ds(pl.multiple_of(to * height, height), height), jrange(j)],
                    dst_ref=out.at[:, place],
                    send_sem=osend.at[j, step],
                    recv_sem=orecv.at[j, step],
                    device_id={"dp": to},
                    device_id_type=pl.DeviceIdType.MESH,
                )
            )
        return remote, pltpu.make_async_copy(
            stage.at[mine, jrange(j)], out.at[:, place], orecv.at[j, 0]
        )

    @pl.loop(0, nj)
    def _(j):
        acc[...] = jnp.zeros_like(acc)
        inv = sinv[jrange(j), 0:1]
        scale = colv[jrange(j), 0:1] * (1.0 / STUDENT_TEMP)

        @pl.loop(0, ni)
        def _(i):
            logit = dots(spt[jrange(j), :], i, bot) * inv
            probs = jnp.exp2(logit * (LOG2E / STUDENT_TEMP)) * stot[pl.ds(i, 1), :]
            grad = probs - exps[jrange(j), irange(i)] * rows[pl.ds(i, 1), :] * scale
            low[:, irange(i)] = grad.astype(BF16)
            acc[...] += fold(grad * logit)

        summed = jnp.dot(low[...], z[:, bot : 2 * bot], preferred_element_type=F32)
        dot = jnp.sum(acc[...], axis=1, keepdims=True)
        result = summed * inv - spt[jrange(j), :].astype(F32) * (dot * inv * inv)
        stage[:, jrange(j)] = result.T
        remote, local = out_copies(j)
        for copy in remote:
            copy.start()
        local.start()

    @pl.loop(0, nj)
    def _(j):
        remote, local = out_copies(j)
        for copy in remote:
            copy.wait()
        local.wait()


def head(n, m, z, teacher_cols, student_protos):
    bot, cols = teacher_cols.shape
    crops = z.shape[0]
    jb = min(cols, 256)
    ib = crops // 8
    ni, nj = crops // ib, cols // jb
    sem = pltpu.SemaphoreType.DMA
    return pl.pallas_call(
        functools.partial(head_kernel, n, m, jb, ib),
        out_shape=jax.ShapeDtypeStruct((bot // n, cols * n), F32),
        in_specs=[
            pl.BlockSpec(memory_space=pltpu.VMEM),
            pl.BlockSpec(memory_space=pltpu.VMEM),
            pl.BlockSpec(memory_space=pl.ANY),
        ],
        out_specs=pl.BlockSpec(memory_space=pl.ANY),
        scratch_shapes=[
            pltpu.VMEM((cols, crops), F32),
            pltpu.VMEM((cols, bot), BF16),
            pltpu.VMEM((bot, cols), BF16),
            pltpu.VMEM((cols, bot), BF16),
            pltpu.VMEM((jb, crops), BF16),
            pltpu.VMEM((bot, cols), F32),
            pltpu.VMEM((jb, 128), F32),
            pltpu.VMEM((cols, 128), F32),
            pltpu.VMEM((cols, 128), F32),
            pltpu.VMEM((cols, 128), F32),
            pltpu.VMEM((ITERS, 2 * ni, ib), F32),
            pltpu.VMEM((ITERS, 2 * ni, ib), F32),
            pltpu.VMEM((ITERS, m, 2 * ni, ib), F32),
            pltpu.VMEM((ITERS, n, 2 * ni, ib), F32),
            pltpu.VMEM((ni, ib), F32),
            pltpu.VMEM((ni, ib), F32),
            sem((n,)),
            sem((n,)),
            sem((ITERS, m)),
            sem((ITERS, m)),
            sem((ITERS, n)),
            sem((ITERS, n)),
            sem((nj, n)),
            sem((nj, n)),
        ],
        compiler_params=pltpu.CompilerParams(
            collective_id=1, has_side_effects=True, vmem_limit_bytes=58 * MIB
        ),
    )(z, teacher_cols, student_protos)


def body(n, m, crop_inputs, hidden_weight, hidden_bias, out_weight, out_bias, teacher_feat, student_protos, teacher_protos):
    share = crop_inputs.shape[0] // m
    start = lax.axis_index("proto") * share
    inputs = lax.dynamic_slice_in_dim(crop_inputs, start, share, 0)
    feat = lax.dynamic_slice_in_dim(teacher_feat, start, share, 0)
    student_z = project(inputs, hidden_weight, hidden_bias, out_weight, out_bias)
    teacher_z = normalize_rows(feat.astype(F32)).astype(BF16)
    both = jnp.concatenate([teacher_z, student_z], axis=1)
    teacher_cols = exchange(n, teacher_protos)
    z = lax.all_gather(both, ("dp", "proto"), axis=0, tiled=True)
    return head(n, m, z, teacher_cols, student_protos)


def solution(mesh):
    n, m = mesh.shape["dp"], mesh.shape["proto"]
    return jax.shard_map(
        functools.partial(body, n, m),
        mesh=mesh,
        in_specs=(P("dp", None), P(), P(), P(), P(), P("dp", None), P("dp", "proto"), P("dp", "proto")),
        out_specs=P("dp", "proto"),
        check_vma=False,
    )
```

```python
import functools

import jax
import jax.numpy as jnp
from jax import lax
from jax.experimental import pallas as pl
from jax.experimental.pallas import tpu as pltpu
from jax.sharding import PartitionSpec as P

ITERS = 3
TEACHER_TEMP = 0.07
STUDENT_TEMP = 0.1
LOG2E = 1.4426950408889634
F32 = jnp.float32
BF16 = jnp.bfloat16
MIB = 1024 * 1024


def normalize_rows(values):
    return values * lax.rsqrt(jnp.sum(values * values, axis=-1, keepdims=True) + 1e-06)


def peer(axis, me, step, size):
    return {axis: lax.rem(me + step, size)}


def barrier(groups):
    sem = pltpu.get_barrier_semaphore()
    count = 0
    for axis, me, size in groups:
        for step in range(1, size):
            pl.semaphore_signal(
                sem, inc=1, device_id=peer(axis, me, step, size), device_id_type=pl.DeviceIdType.MESH
            )
            count += 1
    pl.semaphore_wait(sem, count)


def exchange_copies(n, src, dst, send, recv):
    me = lax.axis_index("dp")
    rows, cols = src.shape[0], src.shape[1] // n
    mine = pl.ds(pl.multiple_of(me * rows, rows), rows)
    copies = []
    for step in range(1, n):
        to = lax.rem(me + step, n)
        copies.append(
            pltpu.make_async_remote_copy(
                src_ref=src.at[:, pl.ds(pl.multiple_of(to * cols, cols), cols)],
                dst_ref=dst.at[mine, :],
                send_sem=send.at[step],
                recv_sem=recv.at[step],
                device_id={"dp": to},
                device_id_type=pl.DeviceIdType.MESH,
            )
        )
    own = pltpu.make_async_copy(
        src.at[:, pl.ds(pl.multiple_of(me * cols, cols), cols)], dst.at[mine, :], recv.at[0]
    )
    return copies, own


class Gather:
    def __init__(self, n, m, src, dst, sems):
        self.zs, self.zr, self.ps, self.pr, self.fs, self.fr = sems
        dp, proto = lax.axis_index("dp"), lax.axis_index("proto")
        rows, chips = src.shape[0], m // 2
        chip, core = proto // 2, proto % 2
        sibling = chip * 2 + 1 - core
        own = pl.ds(pl.multiple_of((proto * n + dp) * rows, rows), rows)
        block = lambda p: dst.at[pl.ds(pl.multiple_of(p * (n * rows), n * rows), n * rows), :]
        copy = functools.partial(
            pltpu.make_async_remote_copy, device_id_type=pl.DeviceIdType.MESH
        )
        self.local = pltpu.make_async_copy(src, dst.at[own, :], self.zr.at[0])
        self.first = [
            copy(src, dst.at[own, :], self.zs.at[k], self.zr.at[k], device_id=peer("dp", dp, k, n))
            for k in range(1, n)
        ]
        self.second = [
            copy(
                block(proto), block(proto), self.ps.at[k], self.pr.at[k],
                device_id={"proto": lax.rem(chip + k, chips) * 2 + core if k else sibling},
            )
            for k in range(chips)
        ]
        self.third = []
        for k in range(1, chips):
            came = lax.rem(chip + chips - k, chips) * 2 + core
            self.third.append(
                copy(block(came), block(came), self.fs.at[k], self.fr.at[k], device_id={"proto": sibling})
            )

    def start(self):
        for copy in self.first:
            copy.start()
        self.local.start()

    def across_chips(self):
        self.local.wait()
        for copy in self.first:
            copy.wait()
        for k in list(range(1, len(self.second))) + [0]:
            self.second[k].start()

    def across_cores(self):
        for k in range(1, len(self.second)):
            self.second[k].wait_recv()
            self.third[k - 1].start()

    def finish(self):
        self.second[0].wait()
        for copy in self.second[1:]:
            copy.wait_send()
        for copy in self.third:
            copy.wait()

    @staticmethod
    def scratch(n, m):
        sem = pltpu.SemaphoreType.DMA
        return [sem((n,)), sem((n,)), sem((m // 2,)), sem((m // 2,)), sem((m // 2,)), sem((m // 2,))]


def input_kernel(
    n, m, kb,
    protos, feat, crops, weight, bias, out_weight, out_bias,
    cols, z, student,
    tz, hw, x, hidden, xs, xr, ls, ws, *gs,
):
    dp, proto = lax.axis_index("dp"), lax.axis_index("proto")
    rows = x.shape[0]
    share = pl.ds(pl.multiple_of(proto * rows, rows), rows)
    load_feat = pltpu.make_async_copy(feat.at[share, :], tz, ls.at[0])
    load_x = pltpu.make_async_copy(crops.at[share, :], x, ls.at[1])

    def columns(k):
        return pl.ds(pl.multiple_of(k * kb, kb), kb)

    def load_weight(k):
        return pltpu.make_async_copy(weight.at[:, columns(k)], hw.at[:, columns(k)], ws.at[k])

    nk = weight.shape[1] // kb
    load_feat.start()
    load_x.start()

    @pl.loop(0, nk)
    def _(k):
        load_weight(k).start()

    barrier([("dp", dp, n), ("proto", proto, m)])
    load_feat.wait()
    tz[...] = normalize_rows(tz[...].astype(F32)).astype(BF16)
    gather = Gather(n, m, tz, z, gs)
    gather.start()
    copies, own = exchange_copies(n, protos, cols, xs, xr)
    for copy in copies:
        copy.start()
    own.start()
    load_x.wait()

    def hidden_columns(k):
        load_weight(k).wait()
        value = jnp.dot(x[...], hw[:, columns(k)], preferred_element_type=F32) + bias[:, columns(k)]
        value = 0.5 * value * (1.0 + lax.erf(value * (0.5 ** 0.5)))
        hidden[:, columns(k)] = value.astype(BF16)

    pl.loop(0, nk // 2)(hidden_columns)
    gather.across_chips()
    pl.loop(nk // 2, nk)(hidden_columns)
    bottle = jnp.dot(hidden[...], out_weight[...], preferred_element_type=F32) + out_bias[...]
    student[...] = normalize_rows(bottle).astype(BF16)
    gather.across_cores()
    gather.finish()
    own.wait()
    for copy in copies:
        copy.wait()


def inputs(n, m, protos, feat, crops, weight, bias, out_weight, out_bias):
    bot, cols = protos.shape[0] * n, protos.shape[1] // n
    rows, width, hid = crops.shape[0] // m, crops.shape[1], weight.shape[1]
    kb = 256
    sem = pltpu.SemaphoreType.DMA
    any_ref, vmem = pl.BlockSpec(memory_space=pl.ANY), pl.BlockSpec(memory_space=pltpu.VMEM)
    return pl.pallas_call(
        functools.partial(input_kernel, n, m, kb),
        out_shape=(
            jax.ShapeDtypeStruct((bot, cols), BF16),
            jax.ShapeDtypeStruct((rows * m * n, bot), BF16),
            jax.ShapeDtypeStruct((rows, bot), BF16),
        ),
        in_specs=[any_ref, any_ref, any_ref, any_ref, vmem, vmem, vmem],
        out_specs=(any_ref, any_ref, vmem),
        scratch_shapes=[
            pltpu.VMEM((rows, bot), BF16),
            pltpu.VMEM((width, hid), BF16),
            pltpu.VMEM((rows, width), BF16),
            pltpu.VMEM((rows, hid), BF16),
            sem((n,)),
            sem((n,)),
            sem((2,)),
            sem((hid // kb,)),
            *Gather.scratch(n, m),
        ],
        compiler_params=pltpu.CompilerParams(
            collective_id=0, has_side_effects=True, vmem_limit_bytes=58 * MIB
        ),
    )(protos, feat, crops, weight, bias[None, :], out_weight, out_bias[None, :])


def head_kernel(
    n, m, jb, ib,
    tz, tp, mine_z, sp, out,
    sz, exps, tpt, sps, spt, low, stage, acc, tcoef, sinv, colv,
    part, part2, from_proto, from_dp, rows, stot,
    xsend, xrecv, psend, precv, dsend, drecv, osend, orecv, *gs,
):
    dp, proto = lax.axis_index("dp"), lax.axis_index("proto")
    bot, cols = tp.shape
    crops = tz.shape[0]
    nj, ni = cols // jb, crops // ib
    lanes = 128

    barrier([("dp", dp, n), ("proto", proto, m)])
    gather = Gather(n, m, mine_z, sz, gs)
    gather.start()
    copies, own = exchange_copies(n, sp, sps, xsend, xrecv)
    for copy in copies:
        copy.start()
    own.start()

    def jrange(j):
        return pl.ds(pl.multiple_of(j * jb, jb), jb)

    def irange(i):
        return pl.ds(pl.multiple_of(i * ib, ib), ib)

    def prepare(src, dst, coef, factor):
        @pl.loop(0, nj)
        def _(j):
            block = src[:, jrange(j)].T
            dst[jrange(j), :] = block
            wide = block.astype(F32)
            inv = lax.rsqrt(jnp.sum(wide * wide, axis=1, keepdims=True) + 1e-06) * factor
            coef[jrange(j), :] = jnp.broadcast_to(inv, (jb, lanes))

    def dots(protos, i, z):
        return lax.dot_general(
            protos, z[irange(i), :], (((1,), (1,)), ((), ())),
            preferred_element_type=F32,
        )

    def fold(values):
        total = values[:, :lanes]
        for k in range(1, ib // lanes):
            total = total + values[:, k * lanes : (k + 1) * lanes]
        return total

    def add_rows(j, slot):
        scale = 1.0 / jnp.sum(acc[...], axis=1, keepdims=True)
        colv[jrange(j), :] = jnp.broadcast_to(scale, (jb, lanes))

        @pl.loop(0, ni)
        def _(i):
            part[slot, pl.ds(i, 1), :] += jnp.sum(
                exps[jrange(j), irange(i)] * scale, axis=0, keepdims=True
            )

    def reduce_copies(axis, me, size, src, dst, send, recv, slot, height):
        return [
            pltpu.make_async_remote_copy(
                src_ref=src.at[slot, pl.ds(0, height), :],
                dst_ref=dst.at[slot, step, pl.ds(0, height), :],
                send_sem=send.at[slot, step],
                recv_sem=recv.at[slot, step],
                device_id=peer(axis, me, step, size),
                device_id_type=pl.DeviceIdType.MESH,
            )
            for step in range(1, size)
        ]

    def reduce_all(slot, height, fillers):
        first = reduce_copies("proto", proto, m, part, from_proto, psend, precv, slot, height)
        for copy in first:
            copy.start()
        fillers[0]()
        for copy in first:
            copy.wait()
        total = part[slot, 0:height, :]
        for step in range(1, m):
            total = total + from_proto[slot, step, 0:height, :]
        part2[slot, 0:height, :] = total
        second = reduce_copies("dp", dp, n, part2, from_dp, dsend, drecv, slot, height)
        for copy in second:
            copy.start()
        fillers[1]()
        for copy in second:
            copy.wait()
        total = part2[slot, 0:height, :]
        for step in range(1, n):
            total = total + from_dp[slot, step, 0:height, :]
        return total

    def nothing():
        pass

    part[...] = jnp.zeros_like(part)
    prepare(tp, tpt, tcoef, LOG2E / TEACHER_TEMP)

    def teacher_block(j):
        acc[...] = jnp.zeros_like(acc)
        coef = tcoef[jrange(j), 0:1]

        @pl.loop(0, ni)
        def _(i):
            block = jnp.exp2(dots(tpt[jrange(j), :], i, tz) * coef)
            exps[jrange(j), irange(i)] = block
            acc[...] += fold(block)

        add_rows(j, 0)

    pl.loop(0, nj // 2)(teacher_block)
    gather.across_chips()
    pl.loop(nj // 2, nj)(teacher_block)

    def student_totals(first, last):
        @pl.loop(first, last)
        def _(j):
            coef = sinv[jrange(j), 0:1] * (LOG2E / STUDENT_TEMP)

            @pl.loop(0, ni)
            def _(i):
                block = jnp.exp2(dots(spt[jrange(j), :], i, sz) * coef)
                part[2, pl.ds(ni + i, 1), :] += jnp.sum(block, axis=0, keepdims=True)

    def student_first():
        gather.finish()
        own.wait()
        for copy in copies:
            copy.wait()
        prepare(sps, spt, sinv, 1.0)
        student_totals(0, nj // 2)

    def student_second():
        student_totals(nj // 2, nj)

    for slot in range(ITERS):
        last = slot == ITERS - 1
        fillers = ((gather.across_cores, nothing), (student_first, student_second), (nothing, nothing))[slot]
        total = reduce_all(slot, 2 * ni if last else ni, fillers)
        rows[...] = 1.0 / total[0:ni, :]
        if last:
            stot[...] = (1.0 / STUDENT_TEMP) / total[ni : 2 * ni, :]
            break

        @pl.loop(0, nj)
        def _(j):
            acc[...] = jnp.zeros_like(acc)

            @pl.loop(0, ni)
            def _(i):
                acc[...] += fold(exps[jrange(j), irange(i)] * rows[pl.ds(i, 1), :])

            add_rows(j, slot + 1)

    height = bot // n
    mine = pl.ds(pl.multiple_of(dp * height, height), height)

    def out_copies(j):
        place = pl.ds(pl.multiple_of(dp * cols + j * jb, jb), jb)
        remote = []
        for step in range(1, n):
            to = lax.rem(dp + step, n)
            remote.append(
                pltpu.make_async_remote_copy(
                    src_ref=stage.at[pl.ds(pl.multiple_of(to * height, height), height), jrange(j)],
                    dst_ref=out.at[:, place],
                    send_sem=osend.at[j, step],
                    recv_sem=orecv.at[j, step],
                    device_id={"dp": to},
                    device_id_type=pl.DeviceIdType.MESH,
                )
            )
        return remote, pltpu.make_async_copy(
            stage.at[mine, jrange(j)], out.at[:, place], orecv.at[j, 0]
        )

    @pl.loop(0, nj)
    def _(j):
        acc[...] = jnp.zeros_like(acc)
        inv = sinv[jrange(j), 0:1]
        scale = colv[jrange(j), 0:1] * (1.0 / STUDENT_TEMP)

        @pl.loop(0, ni)
        def _(i):
            logit = dots(spt[jrange(j), :], i, sz) * inv
            probs = jnp.exp2(logit * (LOG2E / STUDENT_TEMP)) * stot[pl.ds(i, 1), :]
            grad = probs - exps[jrange(j), irange(i)] * rows[pl.ds(i, 1), :] * scale
            low[:, irange(i)] = grad.astype(BF16)
            acc[...] += fold(grad * logit)

        summed = jnp.dot(low[...], sz[...], preferred_element_type=F32)
        dot = jnp.sum(acc[...], axis=1, keepdims=True)
        result = summed * inv - spt[jrange(j), :].astype(F32) * (dot * inv * inv)
        stage[:, jrange(j)] = result.T
        remote, local = out_copies(j)
        for copy in remote:
            copy.start()
        local.start()

    @pl.loop(0, nj)
    def _(j):
        remote, local = out_copies(j)
        for copy in remote:
            copy.wait()
        local.wait()


def head(n, m, teacher_z, teacher_cols, student_z, student_protos):
    bot, cols = teacher_cols.shape
    crops = teacher_z.shape[0]
    jb = min(cols, 256)
    ib = crops // 8
    ni, nj = crops // ib, cols // jb
    sem = pltpu.SemaphoreType.DMA
    return pl.pallas_call(
        functools.partial(head_kernel, n, m, jb, ib),
        out_shape=jax.ShapeDtypeStruct((bot // n, cols * n), F32),
        in_specs=[
            pl.BlockSpec(memory_space=pltpu.VMEM),
            pl.BlockSpec(memory_space=pltpu.VMEM),
            pl.BlockSpec(memory_space=pltpu.VMEM),
            pl.BlockSpec(memory_space=pl.ANY),
        ],
        out_specs=pl.BlockSpec(memory_space=pl.ANY),
        scratch_shapes=[
            pltpu.VMEM((crops, bot), BF16),
            pltpu.VMEM((cols, crops), F32),
            pltpu.VMEM((cols, bot), BF16),
            pltpu.VMEM((bot, cols), BF16),
            pltpu.VMEM((cols, bot), BF16),
            pltpu.VMEM((jb, crops), BF16),
            pltpu.VMEM((bot, cols), F32),
            pltpu.VMEM((jb, 128), F32),
            pltpu.VMEM((cols, 128), F32),
            pltpu.VMEM((cols, 128), F32),
            pltpu.VMEM((cols, 128), F32),
            pltpu.VMEM((ITERS, 2 * ni, ib), F32),
            pltpu.VMEM((ITERS, 2 * ni, ib), F32),
            pltpu.VMEM((ITERS, m, 2 * ni, ib), F32),
            pltpu.VMEM((ITERS, n, 2 * ni, ib), F32),
            pltpu.VMEM((ni, ib), F32),
            pltpu.VMEM((ni, ib), F32),
            sem((n,)),
            sem((n,)),
            sem((ITERS, m)),
            sem((ITERS, m)),
            sem((ITERS, n)),
            sem((ITERS, n)),
            sem((nj, n)),
            sem((nj, n)),
            *Gather.scratch(n, m),
        ],
        compiler_params=pltpu.CompilerParams(
            collective_id=1, has_side_effects=True, vmem_limit_bytes=58 * MIB
        ),
    )(teacher_z, teacher_cols, student_z, student_protos)


def body(n, m, crop_inputs, hidden_weight, hidden_bias, out_weight, out_bias, teacher_feat, student_protos, teacher_protos):
    teacher_cols, teacher_z, student_z = inputs(
        n, m, teacher_protos, teacher_feat, crop_inputs, hidden_weight, hidden_bias, out_weight, out_bias
    )
    return head(n, m, teacher_z, teacher_cols, student_z, student_protos)


def solution(mesh):
    n, m = mesh.shape["dp"], mesh.shape["proto"]
    return jax.shard_map(
        functools.partial(body, n, m),
        mesh=mesh,
        in_specs=(P("dp", None), P(), P(), P(), P(), P("dp", None), P("dp", "proto"), P("dp", "proto")),
        out_specs=P("dp", "proto"),
        check_vma=False,
    )
```

```python
import functools

import jax
import jax.numpy as jnp
from jax import lax
from jax.experimental import pallas as pl
from jax.experimental.pallas import tpu as pltpu
from jax.sharding import PartitionSpec as P

ITERS = 3
TEACHER_TEMP = 0.07
STUDENT_TEMP = 0.1
LOG2E = 1.4426950408889634
F32 = jnp.float32
BF16 = jnp.bfloat16
MIB = 1024 * 1024


def normalize_rows(values):
    return values * lax.rsqrt(jnp.sum(values * values, axis=-1, keepdims=True) + 1e-06)


def peer(axis, me, step, size):
    return {axis: lax.rem(me + step, size)}


def barrier(groups):
    sem = pltpu.get_barrier_semaphore()
    count = 0
    for axis, me, size in groups:
        for step in range(1, size):
            pl.semaphore_signal(
                sem, inc=1, device_id=peer(axis, me, step, size), device_id_type=pl.DeviceIdType.MESH
            )
            count += 1
    pl.semaphore_wait(sem, count)


def exchange_copies(n, src, dst, send, recv):
    me = lax.axis_index("dp")
    rows, cols = src.shape[0], src.shape[1] // n
    mine = pl.ds(pl.multiple_of(me * rows, rows), rows)
    copies = []
    for step in range(1, n):
        to = lax.rem(me + step, n)
        copies.append(
            pltpu.make_async_remote_copy(
                src_ref=src.at[:, pl.ds(pl.multiple_of(to * cols, cols), cols)],
                dst_ref=dst.at[mine, :],
                send_sem=send.at[step],
                recv_sem=recv.at[step],
                device_id={"dp": to},
                device_id_type=pl.DeviceIdType.MESH,
            )
        )
    own = pltpu.make_async_copy(
        src.at[:, pl.ds(pl.multiple_of(me * cols, cols), cols)], dst.at[mine, :], recv.at[0]
    )
    return copies, own


class Gather:
    def __init__(self, n, m, src, dst, sems):
        self.zs, self.zr, self.ps, self.pr, self.fs, self.fr = sems
        dp, proto = lax.axis_index("dp"), lax.axis_index("proto")
        rows, chips = src.shape[0], m // 2
        chip, core = proto // 2, proto % 2
        sibling = chip * 2 + 1 - core
        own = pl.ds(pl.multiple_of((proto * n + dp) * rows, rows), rows)
        block = lambda p: dst.at[pl.ds(pl.multiple_of(p * (n * rows), n * rows), n * rows), :]
        copy = functools.partial(
            pltpu.make_async_remote_copy, device_id_type=pl.DeviceIdType.MESH
        )
        self.local = pltpu.make_async_copy(src, dst.at[own, :], self.zr.at[0])
        self.first = [
            copy(src, dst.at[own, :], self.zs.at[k], self.zr.at[k], device_id=peer("dp", dp, k, n))
            for k in range(1, n)
        ]
        self.second = [
            copy(
                block(proto), block(proto), self.ps.at[k], self.pr.at[k],
                device_id={"proto": lax.rem(chip + k, chips) * 2 + core if k else sibling},
            )
            for k in range(chips)
        ]
        self.third = []
        for k in range(1, chips):
            came = lax.rem(chip + chips - k, chips) * 2 + core
            self.third.append(
                copy(block(came), block(came), self.fs.at[k], self.fr.at[k], device_id={"proto": sibling})
            )

    def start(self):
        for copy in self.first:
            copy.start()
        self.local.start()

    def across_chips(self):
        self.local.wait()
        for copy in self.first:
            copy.wait()
        for k in list(range(1, len(self.second))) + [0]:
            self.second[k].start()

    def across_cores(self):
        for k in range(1, len(self.second)):
            self.second[k].wait_recv()
            self.third[k - 1].start()

    def finish(self):
        self.second[0].wait()
        for copy in self.second[1:]:
            copy.wait_send()
        for copy in self.third:
            copy.wait()

    @staticmethod
    def scratch(n, m):
        sem = pltpu.SemaphoreType.DMA
        return [sem((n,)), sem((n,)), sem((m // 2,)), sem((m // 2,)), sem((m // 2,)), sem((m // 2,))]


def input_kernel(
    n, m, kb,
    protos, feat, crops, weight, bias, out_weight, out_bias,
    cols, z, student,
    tz, hw, x, hidden, xs, xr, ls, ws, *gs,
):
    dp, proto = lax.axis_index("dp"), lax.axis_index("proto")
    rows = x.shape[0]
    share = pl.ds(pl.multiple_of(proto * rows, rows), rows)
    load_feat = pltpu.make_async_copy(feat.at[share, :], tz, ls.at[0])
    load_x = pltpu.make_async_copy(crops.at[share, :], x, ls.at[1])

    def columns(k):
        return pl.ds(pl.multiple_of(k * kb, kb), kb)

    def load_weight(k):
        return pltpu.make_async_copy(weight.at[:, columns(k)], hw.at[:, columns(k)], ws.at[k])

    nk = weight.shape[1] // kb
    load_feat.start()
    load_x.start()

    @pl.loop(0, nk)
    def _(k):
        load_weight(k).start()

    barrier([("dp", dp, n), ("proto", proto, m)])
    load_feat.wait()
    tz[...] = normalize_rows(tz[...].astype(F32)).astype(BF16)
    gather = Gather(n, m, tz, z, gs)
    gather.start()
    copies, own = exchange_copies(n, protos, cols, xs, xr)
    for copy in copies:
        copy.start()
    own.start()
    load_x.wait()

    def hidden_columns(k):
        load_weight(k).wait()
        value = jnp.dot(x[...], hw[:, columns(k)], preferred_element_type=F32) + bias[:, columns(k)]
        value = 0.5 * value * (1.0 + lax.erf(value * (0.5 ** 0.5)))
        hidden[:, columns(k)] = value.astype(BF16)

    pl.loop(0, nk // 2)(hidden_columns)
    gather.across_chips()
    pl.loop(nk // 2, nk)(hidden_columns)
    bottle = jnp.dot(hidden[...], out_weight[...], preferred_element_type=F32) + out_bias[...]
    student[...] = normalize_rows(bottle).astype(BF16)
    gather.across_cores()
    gather.finish()
    own.wait()
    for copy in copies:
        copy.wait()


def inputs(n, m, protos, feat, crops, weight, bias, out_weight, out_bias):
    bot, cols = protos.shape[0] * n, protos.shape[1] // n
    rows, width, hid = crops.shape[0] // m, crops.shape[1], weight.shape[1]
    kb = 256
    sem = pltpu.SemaphoreType.DMA
    any_ref, vmem = pl.BlockSpec(memory_space=pl.ANY), pl.BlockSpec(memory_space=pltpu.VMEM)
    return pl.pallas_call(
        functools.partial(input_kernel, n, m, kb),
        out_shape=(
            jax.ShapeDtypeStruct((bot, cols), BF16),
            jax.ShapeDtypeStruct((rows * m * n, bot), BF16),
            jax.ShapeDtypeStruct((rows, bot), BF16),
        ),
        in_specs=[any_ref, any_ref, any_ref, any_ref, vmem, vmem, vmem],
        out_specs=(any_ref, any_ref, vmem),
        scratch_shapes=[
            pltpu.VMEM((rows, bot), BF16),
            pltpu.VMEM((width, hid), BF16),
            pltpu.VMEM((rows, width), BF16),
            pltpu.VMEM((rows, hid), BF16),
            sem((n,)),
            sem((n,)),
            sem((2,)),
            sem((hid // kb,)),
            *Gather.scratch(n, m),
        ],
        compiler_params=pltpu.CompilerParams(
            collective_id=0, has_side_effects=True, vmem_limit_bytes=58 * MIB
        ),
    )(protos, feat, crops, weight, bias[None, :], out_weight, out_bias[None, :])


def head_kernel(
    n, m, jb, fb, ib,
    tz, tp, mine_z, sp, out,
    sz, exps, tpt, sps, spt, low, stage, acc, tcoef, sinv, colv,
    part, part2, from_proto, from_dp, rows, stot,
    xsend, xrecv, psend, precv, dsend, drecv, osend, orecv, *gs,
):
    dp, proto = lax.axis_index("dp"), lax.axis_index("proto")
    bot, cols = tp.shape
    crops = tz.shape[0]
    nj, ni = cols // jb, crops // ib
    lanes = 128

    barrier([("dp", dp, n), ("proto", proto, m)])
    gather = Gather(n, m, mine_z, sz, gs)
    gather.start()
    copies, own = exchange_copies(n, sp, sps, xsend, xrecv)
    for copy in copies:
        copy.start()
    own.start()

    def jrange(j):
        return pl.ds(pl.multiple_of(j * jb, jb), jb)

    def irange(i):
        return pl.ds(pl.multiple_of(i * ib, ib), ib)

    def prepare(src, dst, coef, factor):
        @pl.loop(0, nj)
        def _(j):
            block = src[:, jrange(j)].T
            dst[jrange(j), :] = block
            wide = block.astype(F32)
            inv = lax.rsqrt(jnp.sum(wide * wide, axis=1, keepdims=True) + 1e-06) * factor
            coef[jrange(j), :] = jnp.broadcast_to(inv, (jb, lanes))

    def dots(protos, i, z):
        return lax.dot_general(
            protos, z[irange(i), :], (((1,), (1,)), ((), ())),
            preferred_element_type=F32,
        )

    def fold(values):
        total = values[:, :lanes]
        for k in range(1, ib // lanes):
            total = total + values[:, k * lanes : (k + 1) * lanes]
        return total

    def add_rows(j, slot):
        scale = 1.0 / jnp.sum(acc[...], axis=1, keepdims=True)
        colv[jrange(j), :] = jnp.broadcast_to(scale, (jb, lanes))

        @pl.loop(0, ni)
        def _(i):
            part[slot, pl.ds(i, 1), :] += jnp.sum(
                exps[jrange(j), irange(i)] * scale, axis=0, keepdims=True
            )

    def reduce_copies(axis, me, size, src, dst, send, recv, slot, height):
        return [
            pltpu.make_async_remote_copy(
                src_ref=src.at[slot, pl.ds(0, height), :],
                dst_ref=dst.at[slot, step, pl.ds(0, height), :],
                send_sem=send.at[slot, step],
                recv_sem=recv.at[slot, step],
                device_id=peer(axis, me, step, size),
                device_id_type=pl.DeviceIdType.MESH,
            )
            for step in range(1, size)
        ]

    def reduce_all(slot, height, fillers):
        first = reduce_copies("proto", proto, m, part, from_proto, psend, precv, slot, height)
        for copy in first:
            copy.start()
        fillers[0]()
        for copy in first:
            copy.wait()
        total = part[slot, 0:height, :]
        for step in range(1, m):
            total = total + from_proto[slot, step, 0:height, :]
        part2[slot, 0:height, :] = total
        second = reduce_copies("dp", dp, n, part2, from_dp, dsend, drecv, slot, height)
        for copy in second:
            copy.start()
        fillers[1]()
        for copy in second:
            copy.wait()
        total = part2[slot, 0:height, :]
        for step in range(1, n):
            total = total + from_dp[slot, step, 0:height, :]
        return total

    def nothing():
        pass

    part[...] = jnp.zeros_like(part)
    prepare(tp, tpt, tcoef, LOG2E / TEACHER_TEMP)

    def teacher_block(j):
        acc[...] = jnp.zeros_like(acc)
        coef = tcoef[jrange(j), 0:1]

        @pl.loop(0, ni)
        def _(i):
            block = jnp.exp2(dots(tpt[jrange(j), :], i, tz) * coef)
            exps[jrange(j), irange(i)] = block
            acc[...] += fold(block)

        add_rows(j, 0)

    pl.loop(0, nj // 2)(teacher_block)
    gather.across_chips()
    pl.loop(nj // 2, nj)(teacher_block)

    def student_totals(first, last):
        @pl.loop(first, last)
        def _(j):
            coef = sinv[jrange(j), 0:1] * (LOG2E / STUDENT_TEMP)

            @pl.loop(0, ni)
            def _(i):
                block = jnp.exp2(dots(spt[jrange(j), :], i, sz) * coef)
                part[2, pl.ds(ni + i, 1), :] += jnp.sum(block, axis=0, keepdims=True)

    def student_first():
        gather.finish()
        own.wait()
        for copy in copies:
            copy.wait()
        prepare(sps, spt, sinv, 1.0)
        student_totals(0, nj // 4)

    def student_second():
        student_totals(nj // 4, 3 * nj // 4)

    def student_third():
        student_totals(3 * nj // 4, nj)

    for slot in range(ITERS):
        last = slot == ITERS - 1
        fillers = ((gather.across_cores, student_first), (student_second, student_third), (nothing, nothing))[slot]
        total = reduce_all(slot, 2 * ni if last else ni, fillers)
        rows[...] = 1.0 / total[0:ni, :]
        if last:
            stot[...] = (1.0 / STUDENT_TEMP) / total[ni : 2 * ni, :]
            break

        @pl.loop(0, nj)
        def _(j):
            acc[...] = jnp.zeros_like(acc)

            @pl.loop(0, ni)
            def _(i):
                acc[...] += fold(exps[jrange(j), irange(i)] * rows[pl.ds(i, 1), :])

            add_rows(j, slot + 1)

    facc = acc.at[pl.ds(0, fb), :]

    def frange(j):
        return pl.ds(pl.multiple_of(j * fb, fb), fb)

    height = bot // n
    mine = pl.ds(pl.multiple_of(dp * height, height), height)

    def out_copies(j):
        place = pl.ds(pl.multiple_of(dp * cols + j * fb, fb), fb)
        remote = []
        for step in range(1, n):
            to = lax.rem(dp + step, n)
            remote.append(
                pltpu.make_async_remote_copy(
                    src_ref=stage.at[pl.ds(pl.multiple_of(to * height, height), height), frange(j)],
                    dst_ref=out.at[:, place],
                    send_sem=osend.at[j, step],
                    recv_sem=orecv.at[j, step],
                    device_id={"dp": to},
                    device_id_type=pl.DeviceIdType.MESH,
                )
            )
        return remote, pltpu.make_async_copy(
            stage.at[mine, frange(j)], out.at[:, place], orecv.at[j, 0]
        )

    @pl.loop(0, cols // fb)
    def _(j):
        facc[...] = jnp.zeros_like(facc)
        inv = sinv[frange(j), 0:1]
        scale = colv[frange(j), 0:1] * (1.0 / STUDENT_TEMP)

        @pl.loop(0, ni)
        def _(i):
            logit = dots(spt[frange(j), :], i, sz) * inv
            probs = jnp.exp2(logit * (LOG2E / STUDENT_TEMP)) * stot[pl.ds(i, 1), :]
            grad = probs - exps[frange(j), irange(i)] * rows[pl.ds(i, 1), :] * scale
            low[:, irange(i)] = grad.astype(BF16)
            facc[...] += fold(grad * logit)

        summed = jnp.dot(low[...], sz[...], preferred_element_type=F32)
        dot = jnp.sum(facc[...], axis=1, keepdims=True)
        result = summed * inv - spt[frange(j), :].astype(F32) * (dot * inv * inv)
        stage[:, frange(j)] = result.T
        remote, local = out_copies(j)
        for copy in remote:
            copy.start()
        local.start()

    @pl.loop(0, cols // fb)
    def _(j):
        remote, local = out_copies(j)
        for copy in remote:
            copy.wait()
        local.wait()


def head(n, m, teacher_z, teacher_cols, student_z, student_protos):
    bot, cols = teacher_cols.shape
    crops = teacher_z.shape[0]
    jb, fb = min(cols, 1024), min(cols, 256)
    ib = crops // 8
    ni = crops // ib
    sem = pltpu.SemaphoreType.DMA
    return pl.pallas_call(
        functools.partial(head_kernel, n, m, jb, fb, ib),
        out_shape=jax.ShapeDtypeStruct((bot // n, cols * n), F32),
        in_specs=[
            pl.BlockSpec(memory_space=pltpu.VMEM),
            pl.BlockSpec(memory_space=pltpu.VMEM),
            pl.BlockSpec(memory_space=pltpu.VMEM),
            pl.BlockSpec(memory_space=pl.ANY),
        ],
        out_specs=pl.BlockSpec(memory_space=pl.ANY),
        scratch_shapes=[
            pltpu.VMEM((crops, bot), BF16),
            pltpu.VMEM((cols, crops), F32),
            pltpu.VMEM((cols, bot), BF16),
            pltpu.VMEM((bot, cols), BF16),
            pltpu.VMEM((cols, bot), BF16),
            pltpu.VMEM((fb, crops), BF16),
            pltpu.VMEM((bot, cols), F32),
            pltpu.VMEM((jb, 128), F32),
            pltpu.VMEM((cols, 128), F32),
            pltpu.VMEM((cols, 128), F32),
            pltpu.VMEM((cols, 128), F32),
            pltpu.VMEM((ITERS, 2 * ni, ib), F32),
            pltpu.VMEM((ITERS, 2 * ni, ib), F32),
            pltpu.VMEM((ITERS, m, 2 * ni, ib), F32),
            pltpu.VMEM((ITERS, n, 2 * ni, ib), F32),
            pltpu.VMEM((ni, ib), F32),
            pltpu.VMEM((ni, ib), F32),
            sem((n,)),
            sem((n,)),
            sem((ITERS, m)),
            sem((ITERS, m)),
            sem((ITERS, n)),
            sem((ITERS, n)),
            sem((cols // fb, n)),
            sem((cols // fb, n)),
            *Gather.scratch(n, m),
        ],
        compiler_params=pltpu.CompilerParams(
            collective_id=1, has_side_effects=True, vmem_limit_bytes=58 * MIB
        ),
    )(teacher_z, teacher_cols, student_z, student_protos)


def body(n, m, crop_inputs, hidden_weight, hidden_bias, out_weight, out_bias, teacher_feat, student_protos, teacher_protos):
    teacher_cols, teacher_z, student_z = inputs(
        n, m, teacher_protos, teacher_feat, crop_inputs, hidden_weight, hidden_bias, out_weight, out_bias
    )
    return head(n, m, teacher_z, teacher_cols, student_z, student_protos)


def solution(mesh):
    n, m = mesh.shape["dp"], mesh.shape["proto"]
    return jax.shard_map(
        functools.partial(body, n, m),
        mesh=mesh,
        in_specs=(P("dp", None), P(), P(), P(), P(), P("dp", None), P("dp", "proto"), P("dp", "proto")),
        out_specs=P("dp", "proto"),
        check_vma=False,
    )
```
